512 devices in a mesh: section: 4 (over x_lo, core), fsdp: 32 (over x_hi, z), tensor: 4 (over y).
Axes of the slice: x: 4 (x_hi: 2, x_lo: 2; x = x_hi * 2 + x_lo), y: 4, z: 16, core: 2. Of those that a mesh axis runs over, the one named last changes fastest.
Arguments:
- entering: bfloat16 [4, 16384, 2048], P('section', 'fsdp', 'tensor'), may hold values from -8 to 8
- w_query: bfloat16 [4, 2048, 4096], P('section', 'fsdp', 'tensor'), may hold values from -0.125 to 0.125
- w_keyval: bfloat16 [4, 2048, 4, 256], P('section', 'fsdp', 'tensor'), may hold values from -0.125 to 0.125
- w_out: bfloat16 [4, 4096, 2048], P('section', 'tensor', 'fsdp'), may hold values from -0.09375 to 0.09375
Outputs:
- leaving: bfloat16 [4, 16384, 2048], P('section', 'fsdp', 'tensor')
The draws below stay inside these ranges and needn't reach their ends.
All inputs are finite; a program needn't handle non-finite values.
Results may differ from the reference program's by a relative error of at most 0.0055.
Values may be sent and summed in bfloat16 or wider, within the bound.
A program may use at most 64 MiB of HBM per device.

```python
import math
import jax
import jax.numpy as jnp
from jax import lax

D = 2048
HEADS = 32
KV_HEADS = 4
HEAD_DIM = 128
SEQ = 512
SECTIONS = 4
TOKENS = 16384
N_FSDP = 32
N_TENSOR = 4


def draw_entering(key, part):
    first_key = jax.random.fold_in(key, 0)
    values = jax.random.normal(first_key, (SECTIONS, TOKENS, D), jnp.float32)
    return jnp.clip(values, -8.0, 8.0).astype(jnp.bfloat16)


def block_scale(key, shape, shards, low, high):
    factor_of = 1.0
    for position, blocks in shards:
        draws = jax.random.uniform(jax.random.fold_in(jax.random.fold_in(key, 6), position), (blocks,), jnp.float32, low / len(shards), high / len(shards))
        factor_of = factor_of * jnp.repeat(jnp.exp(draws), shape[position] // blocks).reshape((-1,) + (1,) * (len(shape) - 1 - position))
    return factor_of


def gaussian(key, extent, spread, reach, pieces=(), kind=jnp.bfloat16):
    array = jax.random.normal(key, extent, jnp.float32) * spread
    if len(pieces) > 0:
        array = block_scale(key, extent, pieces, -0.22, 0.18) * array
    return jnp.clip(array, min=-reach, max=reach).astype(kind)


def setup_inputs(seed: int = 0) -> dict:
    seeds = jax.random.split(jax.random.key(seed), 5)
    entering = draw_entering(jax.random.fold_in(seeds[4], 71), 0)
    w_query = gaussian(seeds[1], (SECTIONS, D, HEADS * HEAD_DIM), D ** -0.5, 0.125, ((0, 4), (1, 32), (2, 4)))
    w_keyval = gaussian(seeds[2], (SECTIONS, D, KV_HEADS, 2 * HEAD_DIM), D ** -0.5, 0.125, ((0, 4), (1, 32), (2, 4)))
    w_out = gaussian(seeds[3], (SECTIONS, HEADS * HEAD_DIM, D), (HEADS * HEAD_DIM) ** -0.5, 0.09375, ((0, 4), (1, 4), (2, 32)))
    return {"entering": entering, "w_query": w_query, "w_keyval": w_keyval, "w_out": w_out}


EPSILON = 1e-06
ROPE_BASE = 1000000.0
BEFORE_SHARE = 0.6
AFTER_SHARE = 0.4

def rope_tables(length, width):
    half_width = width // 2
    exponent = jnp.arange(half_width, dtype=jnp.float32) * (2.0 / width)
    inverse = jnp.exp(-exponent * math.log(ROPE_BASE))
    angles = jnp.arange(length, dtype=jnp.float32)[:, None] * inverse[None, :]
    return (jnp.cos(angles)[:, None, :], jnp.sin(angles)[:, None, :])

def head_norm_rope(vectors, cosine, sine):
    meansq = lax.optimization_barrier(jnp.mean(vectors * vectors, axis=-1, keepdims=True))
    normed = vectors * lax.rsqrt(meansq + EPSILON)
    half_width = vectors.shape[-1] // 2
    first_half = normed[..., :half_width]
    second_half = normed[..., half_width:]
    return jnp.concatenate([first_half * cosine - second_half * sine, second_half * cosine + first_half * sine], axis=-1)

def attend(packed):
    queries, keys, values = packed
    length = queries.shape[0]
    scale = 1.0 / math.sqrt(HEAD_DIM)
    scores = jnp.einsum('qkgd,pkd->kgqp', queries.astype(jnp.float32), keys.astype(jnp.float32)) * scale
    positions = jnp.arange(length)
    causal = positions[:, None] >= positions[None, :]
    expo = jnp.where(causal[None, None], jnp.exp(scores - math.sqrt(HEAD_DIM)), 0.0)
    weights = (expo / lax.optimization_barrier(jnp.sum(expo, axis=-1, keepdims=True))).astype(jnp.bfloat16)
    mixed = jnp.einsum('kgqp,pkd->qkgd', weights.astype(jnp.float32), values.astype(jnp.float32))
    return mixed.astype(jnp.bfloat16).reshape(length, -1)

def sublayer(rows, query_weight, keyval_weight, out_weight):
    rows_float = rows.astype(jnp.float32)
    meansq = lax.optimization_barrier(jnp.mean(rows_float * rows_float, axis=-1, keepdims=True))
    normed = (rows_float * lax.rsqrt(meansq + EPSILON)).astype(jnp.bfloat16)
    group_size = HEADS // KV_HEADS
    query_raw = jnp.dot(normed, query_weight, preferred_element_type=jnp.float32)
    query_raw = query_raw.reshape(N_FSDP, SEQ, KV_HEADS, group_size, HEAD_DIM)
    keyval_raw = jnp.dot(normed, keyval_weight.reshape(D, -1), preferred_element_type=jnp.float32)
    keyval_raw = keyval_raw.reshape(N_FSDP, SEQ, KV_HEADS, 2 * HEAD_DIM)
    cosine, sine = rope_tables(SEQ, HEAD_DIM)
    queries = head_norm_rope(query_raw, cosine[:, :, None, :], sine[:, :, None, :]).astype(jnp.bfloat16)
    keys = head_norm_rope(keyval_raw[..., :HEAD_DIM], cosine, sine).astype(jnp.bfloat16)
    values = keyval_raw[..., HEAD_DIM:].astype(jnp.bfloat16)
    mixed = lax.map(attend, (queries, keys, values))
    mixed = mixed.reshape(TOKENS, HEADS * HEAD_DIM)
    shard_width = HEADS * HEAD_DIM // N_TENSOR
    total = jnp.zeros((TOKENS, D), jnp.float32)
    for shard in range(N_TENSOR):
        partial_term = jnp.dot(mixed[:, shard * shard_width:(shard + 1) * shard_width], out_weight[shard * shard_width:(shard + 1) * shard_width], preferred_element_type=jnp.float32).astype(jnp.bfloat16)
        partial_term = lax.optimization_barrier(partial_term)
        total = total + partial_term.astype(jnp.float32)
    return (rows_float + total).astype(jnp.bfloat16)

def rebuild(weights, section):
    lower_part = weights[(section - 1) % SECTIONS].astype(jnp.float32)
    upper_part = weights[(section + 1) % SECTIONS].astype(jnp.float32)
    return (BEFORE_SHARE * lower_part + AFTER_SHARE * upper_part).astype(jnp.bfloat16)

def reference(entering, w_query, w_keyval, w_out):
    results = []
    for section in range(SECTIONS):
        query_weight = rebuild(w_query, section)
        keyval_weight = rebuild(w_keyval, section)
        out_weight = rebuild(w_out, section)
        results.append(sublayer(entering[section], query_weight, keyval_weight, out_weight))
    return jnp.stack(results)
```

```python
import math

import jax
import jax.numpy as jnp
import numpy as np
from jax import lax
from jax.experimental import pallas as pl
from jax.experimental.pallas import tpu as pltpu
from jax.sharding import PartitionSpec as P

HEAD_DIM = 128
EPSILON = 1e-06
ROPE_BASE = 1000000.0
BEFORE_SHARE = 0.6
AFTER_SHARE = 0.4
MESH = pl.DeviceIdType.MESH

ZN = 16
SEC = 4
YN = 4
SEQ = 512
FEAT = 512
ROWS = 64
QE = 512
QL = 768
OE = 512
OL = 512
LOG2E = math.log2(math.e)
NT = (((1,), (1,)), ((), ()))


def rope_tables():
    half = HEAD_DIM // 2
    exponent = np.arange(half, dtype=np.float64) * (2.0 / HEAD_DIM)
    angles = np.arange(SEQ, dtype=np.float64)[:, None] * np.exp(-exponent * math.log(ROPE_BASE))[None, :]
    cosine, sine = np.cos(angles), np.sin(angles)
    return (
        np.concatenate([cosine, cosine], axis=1).astype(np.float32),
        np.concatenate([-sine, sine], axis=1).astype(np.float32),
    )


def kernel(
    e_ref, wq_ref, wkv_ref, wo_ref, cos_ref, sin_ref, out_ref,
    ent, nrm, lo_q, hi_q, lo_kv, hi_kv, lo_o, hi_o, ge, gl, oe, ol,
    qs, ks, vs, mx, pb, rb,
    raw_s, raw_r, ya_s, ya_r, zs, zr, xs, xr, ps, pr,
):
    s, f, t = lax.axis_index("section"), lax.axis_index("fsdp"), lax.axis_index("tensor")
    core = lax.rem(s, 2)
    xh = f // ZN
    z = lax.rem(f, ZN)
    xo = 1 - xh
    fpar = xo * ZN + z
    sec_up, sec_dn = lax.rem(s + 1, SEC), lax.rem(s + SEC - 1, SEC)
    sent = []

    def ydev(j):
        return lax.rem(t + j, YN)

    def zat(x, off):
        return x * ZN + lax.rem(z + 2 * ZN + off, ZN)

    def start(copy):
        copy.start()
        sent.append(copy)

    def remote(src, dst, ss, rs, where):
        return pltpu.make_async_remote_copy(
            src_ref=src, dst_ref=dst, send_sem=ss, recv_sem=rs, device_id=where, device_id_type=MESH
        )

    barrier = pltpu.get_barrier_semaphore()
    peers = [
        (sec_up, f, t), (sec_dn, f, t), (s, fpar, t), (s, zat(xh, 1), t), (s, zat(xh, -1), t),
        (s, f, ydev(1)), (s, f, ydev(2)), (s, f, ydev(3)),
    ]
    for where in peers:
        pl.semaphore_signal(barrier, inc=1, device_id=where, device_id_type=MESH)
    pl.semaphore_wait(barrier, len(peers))

    raw = []
    for i, (src, lo, hi) in enumerate(((wkv_ref, lo_kv, hi_kv), (wq_ref, lo_q, hi_q), (wo_ref, lo_o, hi_o))):
        up = remote(src, lo, raw_s.at[i, 0], raw_r.at[i, 0], (sec_up, f, t))
        dn = remote(src, hi, raw_s.at[i, 1], raw_r.at[i, 1], (sec_dn, f, t))
        start(up)
        start(dn)
        raw.append((up, dn))

    yag = []
    for j in (1, 3, 2):
        start(remote(e_ref, ent.at[t], ya_s.at[j], ya_r.at[j], (s, f, ydev(j))))
        src = lax.rem(t + YN - j, YN)
        yag.append(remote(e_ref, ent.at[src], ya_s.at[j], ya_r.at[j], (s, f, ydev(j))))
    ent[pl.ds(t, 1)] = e_ref[...][None]

    def mix(lo, hi):
        return (BEFORE_SHARE * lo.astype(jnp.float32) + AFTER_SHARE * hi.astype(jnp.float32)).astype(jnp.bfloat16)

    streams = ((ge, xh, None), (gl, xh, 0), (ge, xo, None), (oe, xh, None), (ol, xh, 1), (oe, xo, None))

    def zsend(i, d, k):
        buf, x, _ = streams[i]
        b = zat(x, -d * (k - 1))
        c = 0 if d == 1 else 1
        start(remote(buf.at[b], buf.at[b], zs.at[i, c, k - 1], zr.at[i, c, k - 1], (s, zat(xh, d), t)))

    def zwait(i, d, k):
        buf, x, _ = streams[i]
        b = zat(x, -d * k)
        c = 0 if d == 1 else 1
        remote(buf.at[b], buf.at[b], zs.at[i, c, k - 1], zr.at[i, c, k - 1], (s, zat(xh, d), t)).wait_recv()

    sign = 1 - 2 * core

    def zlast(i):
        buf, x, _ = streams[i]
        b = zat(x, -7 * sign)
        start(remote(buf.at[b], buf.at[b], zs.at[i, 0, 7], zr.at[i, 0, 7], (s, zat(xh, sign), t)))

    def zlast_wait(i):
        buf, x, _ = streams[i]
        b = zat(x, 8)
        remote(buf.at[b], buf.at[b], zs.at[i, 0, 7], zr.at[i, 0, 7], (s, zat(xh, sign), t)).wait_recv()

    def xsend(buf, late, off, slot):
        b = zat(xh, off)
        start(remote(buf.at[b], buf.at[b], xs.at[late, slot], xr.at[late, slot], (s, fpar, t)))

    def xwait(buf, late, off, slot):
        b = zat(xo, off)
        remote(buf.at[b], buf.at[b], xs.at[late, slot], xr.at[late, slot], (s, fpar, t)).wait_recv()

    def slot_of(d, k):
        return k if d == 1 else 7 + k

    def forward(i, d, k):
        buf, _, late = streams[i]
        zwait(i, d, k)
        if k < 7:
            zsend(i, d, k + 1)
        if late is not None:
            xsend(buf, late, -d * k, slot_of(d, k))

    def ring_step(ids, k):
        for i in ids:
            if k < 8:
                forward(i, 1, k)
                forward(i, -1, k)
                if k == 7:
                    zlast(i)
            else:
                zlast_wait(i)
                buf, _, late = streams[i]
                if late is not None:
                    xsend(buf, late, 8, 15)

    def late_wait(buf, late):
        xwait(buf, late, 0, 0)
        for k in range(1, 8):
            xwait(buf, late, -k, slot_of(1, k))
            xwait(buf, late, k, slot_of(-1, k))
        xwait(buf, late, 8, 15)

    for up, dn in raw[:2]:
        up.wait_recv()
        dn.wait_recv()
    ge[pl.ds(f, 1), :, 0:256] = mix(lo_kv[...], hi_kv[...])[None]
    ge[pl.ds(f, 1), :, 256:512] = mix(lo_q[:, 0:256], hi_q[:, 0:256])[None]
    gl[pl.ds(f, 1)] = mix(lo_q[:, 256:1024], hi_q[:, 256:1024])[None]
    xsend(ge, 2, 0, 0)
    for i in (0, 1):
        zsend(i, 1, 1)
        zsend(i, -1, 1)
    xsend(gl, 0, 0, 0)
    raw[2][0].wait_recv()
    raw[2][1].wait_recv()
    oe[pl.ds(f, 1)] = mix(lo_o[:, 0:512], hi_o[:, 0:512])[None]
    ol[pl.ds(f, 1)] = mix(lo_o[:, 512:1024], hi_o[:, 512:1024])[None]
    xsend(oe, 2, 0, 1)
    xwait(ge, 2, 0, 0)
    zsend(2, 1, 1)
    zsend(2, -1, 1)

    def normalise():
        @pl.loop(0, 4)
        def _(m):
            rows = pl.ds(pl.multiple_of(m * 128, 128), 128)
            total = jnp.zeros((128, 1), jnp.float32)
            for c in range(YN):
                block = ent[c, rows, :].astype(jnp.float32)
                total = total + jnp.sum(block * block, axis=1, keepdims=True)
            factor = lax.rsqrt(total * (1.0 / (YN * FEAT)) + EPSILON)
            for c in range(YN):
                block = ent[c, rows, :].astype(jnp.float32)
                nrm[rows, c * FEAT : (c + 1) * FEAT] = (block * factor).astype(jnp.bfloat16)

    for k in range(1, 9):
        ring_step((0, 1, 2), k)
        if k == 3:
            for copy in yag:
                copy.wait_recv()
            normalise()
        if k == 7:
            xwait(oe, 2, 0, 1)
            for i in (3, 4, 5):
                zsend(i, 1, 1)
                zsend(i, -1, 1)
    xsend(ol, 1, 0, 0)
    late_wait(gl, 0)

    def rotate(vectors, rows):
        meansq = jnp.mean(vectors * vectors, axis=-1, keepdims=True)
        normed = vectors * lax.rsqrt(meansq + EPSILON)
        turned = normed * cos_ref[rows, :] + pltpu.roll(normed, 64, 1) * sin_ref[rows, :]
        return turned.astype(jnp.bfloat16)

    def project(src, col, rows):
        weight = src[:, :, pl.ds(col, 256)].reshape(2 * ZN * ROWS, 256)
        return jnp.dot(nrm[rows, :], weight, preferred_element_type=jnp.float32)

    @pl.loop(0, 2)
    def _(m):
        rows = pl.ds(pl.multiple_of(m * 256, 256), 256)
        both = project(ge, 0, rows)
        ks[rows, :] = rotate(both[:, :128], rows)
        vs[rows, :] = both[:, 128:].astype(jnp.bfloat16)
        pair = project(ge, 256, rows)
        qs[0, rows, :] = rotate(pair[:, :128], rows)
        qs[1, rows, :] = rotate(pair[:, 128:], rows)

    def late_queries(n):
        @pl.loop(0, 2)
        def _(m):
            rows = pl.ds(pl.multiple_of(m * 256, 256), 256)
            pair = project(gl, n * 256, rows)
            qs[2 + 2 * n, rows, :] = rotate(pair[:, :128], rows)
            qs[3 + 2 * n, rows, :] = rotate(pair[:, 128:], rows)

    mul = LOG2E / math.sqrt(HEAD_DIM)
    sub = LOG2E * math.sqrt(HEAD_DIM)

    def expo(queries, keys, masked):
        scores = lax.dot_general(queries, keys, NT, preferred_element_type=jnp.float32)
        value = jnp.exp2(scores * mul - sub)
        if masked:
            row = lax.broadcasted_iota(jnp.int32, value.shape, 0)
            col = lax.broadcasted_iota(jnp.int32, value.shape, 1)
            value = jnp.where(row >= col, value, 0.0)
        return value

    def attend(h):
        cols = pl.ds(pl.multiple_of(h * 128, 128), 128)
        e = expo(qs[h, 0:256, :], ks[0:256, :], True)
        w = (e * (1.0 / jnp.sum(e, axis=-1, keepdims=True))).astype(jnp.bfloat16)
        mx[0:256, cols] = jnp.dot(w, vs[0:256, :], preferred_element_type=jnp.float32).astype(jnp.bfloat16)
        queries = qs[h, 256:512, :]
        e0 = expo(queries, ks[0:256, :], False)
        e1 = expo(queries, ks[256:512, :], True)
        r = 1.0 / (jnp.sum(e0, axis=-1, keepdims=True) + jnp.sum(e1, axis=-1, keepdims=True))
        w0 = (e0 * r).astype(jnp.bfloat16)
        w1 = (e1 * r).astype(jnp.bfloat16)
        mixed = jnp.dot(w0, vs[0:256, :], preferred_element_type=jnp.float32)
        mixed = mixed + jnp.dot(w1, vs[256:512, :], preferred_element_type=jnp.float32)
        mx[256:512, cols] = mixed.astype(jnp.bfloat16)

    for k in range(1, 9):
        ring_step((3, 4, 5), k)
        if k in (1, 2, 3):
            late_queries(k - 1)

        if k < 5:
            @pl.loop(0, 2)
            def _(j):
                attend(2 * (k - 1) + j)
    late_wait(ol, 1)

    def partial(target, rows):
        first = oe[pl.ds(target * 8, 8)].reshape(FEAT, OE)
        second = ol[pl.ds(target * 8, 8)].reshape(FEAT, OL)
        value = lax.dot_general(mx[rows, 0:OE], first, NT, preferred_element_type=jnp.float32)
        value = value + lax.dot_general(mx[rows, OE:], second, NT, preferred_element_type=jnp.float32)
        return value.astype(jnp.bfloat16)

    for j in (2, 1, 3):
        @pl.loop(0, 2)
        def _(m):
            rows = pl.ds(pl.multiple_of(m * 256, 256), 256)
            pb[j - 1, rows, :] = partial(ydev(j), rows)
        start(remote(pb.at[j - 1], rb.at[j - 1], ps.at[j - 1], pr.at[j - 1], (s, f, ydev(j))))

    @pl.loop(0, 2)
    def _(m):
        rows = pl.ds(pl.multiple_of(m * 256, 256), 256)
        pb[3, rows, :] = partial(t, rows)
    for j in (2, 1, 3):
        remote(pb.at[j - 1], rb.at[j - 1], ps.at[j - 1], pr.at[j - 1], (s, f, ydev(j))).wait_recv()

    @pl.loop(0, 4)
    def _(m):
        rows = pl.ds(pl.multiple_of(m * 128, 128), 128)
        total = pb[3, rows, :].astype(jnp.float32)
        for j in range(3):
            total = total + rb[j, rows, :].astype(jnp.float32)
        out_ref[rows, :] = (e_ref[rows, :].astype(jnp.float32) + total).astype(jnp.bfloat16)

    for copy in sent:
        copy.wait_send()


def body(entering, w_query, w_keyval, w_out):
    bf16, vmem, dma = jnp.bfloat16, pltpu.VMEM, pltpu.SemaphoreType.DMA
    cosine, sine = rope_tables()
    out = pl.pallas_call(
        kernel,
        out_shape=jax.ShapeDtypeStruct((SEQ, FEAT), bf16),
        in_specs=[pl.BlockSpec(memory_space=vmem)] * 6,
        out_specs=pl.BlockSpec(memory_space=vmem),
        scratch_shapes=[
            vmem((YN, SEQ, FEAT), bf16), vmem((SEQ, YN * FEAT), bf16),
            vmem((ROWS, 1024), bf16), vmem((ROWS, 1024), bf16),
            vmem((ROWS, 256), bf16), vmem((ROWS, 256), bf16),
            vmem((ROWS, 1024), bf16), vmem((ROWS, 1024), bf16),
            vmem((2 * ZN, ROWS, QE), bf16), vmem((2 * ZN, ROWS, QL), bf16),
            vmem((2 * ZN, ROWS, OE), bf16), vmem((2 * ZN, ROWS, OL), bf16),
            vmem((8, SEQ, HEAD_DIM), bf16), vmem((SEQ, HEAD_DIM), bf16), vmem((SEQ, HEAD_DIM), bf16),
            vmem((SEQ, 1024), bf16), vmem((4, SEQ, FEAT), bf16), vmem((3, SEQ, FEAT), bf16),
            dma((3, 2)), dma((3, 2)), dma((4,)), dma((4,)), dma((6, 2, 8)), dma((6, 2, 8)),
            dma((3, 16)), dma((3, 16)), dma((3,)), dma((3,)),
        ],
        compiler_params=pltpu.CompilerParams(
            collective_id=0, has_side_effects=True, vmem_limit_bytes=56 * 1024 * 1024
        ),
        name="section",
    )(
        entering[0], w_query[0], w_keyval.reshape(ROWS, 256), jnp.swapaxes(w_out[0], 0, 1),
        jnp.asarray(cosine), jnp.asarray(sine),
    )
    return out[None]


def solution(mesh):
    in_specs = (
        P("section", "fsdp", "tensor"),
        P("section", "fsdp", "tensor"),
        P("section", "fsdp", "tensor", None),
        P("section", "tensor", "fsdp"),
    )
    out_specs = P("section", "fsdp", "tensor")
    return jax.shard_map(body, mesh=mesh, in_specs=in_specs, out_specs=out_specs, check_vma=False)
```

```python
import math

import jax
import jax.numpy as jnp
import numpy as np
from jax import lax
from jax.experimental import pallas as pl
from jax.experimental.pallas import tpu as pltpu
from jax.sharding import PartitionSpec as P

HEAD_DIM = 128
EPSILON = 1e-06
ROPE_BASE = 1000000.0
BEFORE_SHARE = 0.6
AFTER_SHARE = 0.4
MESH = pl.DeviceIdType.MESH

ZN = 16
SEC = 4
YN = 4
SEQ = 512
FEAT = 512
ROWS = 64
QE = 512
QL = 768
OE = 384
OL = 640
HALF = ROWS // 2
LOG2E = math.log2(math.e)
EARLY = {5: (2, 3), 6: (4, 5), 7: (6,)}
NT = (((1,), (1,)), ((), ()))


def rope_tables():
    half = HEAD_DIM // 2
    exponent = np.arange(half, dtype=np.float64) * (2.0 / HEAD_DIM)
    angles = np.arange(SEQ, dtype=np.float64)[:, None] * np.exp(-exponent * math.log(ROPE_BASE))[None, :]
    cosine, sine = np.cos(angles), np.sin(angles)
    tables = np.concatenate([cosine, cosine], axis=1), np.concatenate([-sine, sine], axis=1)
    return np.stack(tables).astype(np.float32)


def kernel(
    e_hbm, wq_hbm, wkv_hbm, wo_hbm, table_hbm, out_ref,
    ent, nrm, table, raw_e, raw_l, raw_o,
    ge, gl, oe, ol, acc, qs, ks, vs, mx, pb, po, rb, rl,
    local, raw_s, raw_r, ya_s, ya_r, zs, zr, xs, xr, xe_s, xe_r, ps, pr, rr,
):
    s, f, t = lax.axis_index("section"), lax.axis_index("fsdp"), lax.axis_index("tensor")
    core = lax.rem(s, 2)
    xh = f // ZN
    z = lax.rem(f, ZN)
    xo = 1 - xh
    fpar = xo * ZN + z
    sec_up, sec_dn = lax.rem(s + 1, SEC), lax.rem(s + SEC - 1, SEC)

    def ydev(j):
        return lax.rem(t + j, YN)

    def zat(x, off):
        return x * ZN + lax.rem(z + 2 * ZN + off, ZN)

    def remote(src, dst, ss, rs, where):
        return pltpu.make_async_remote_copy(
            src_ref=src, dst_ref=dst, send_sem=ss, recv_sem=rs, device_id=where, device_id_type=MESH
        )

    loads = [
        pltpu.make_async_copy(e_hbm, ent.at[t], local.at[0]),
        pltpu.make_async_copy(table_hbm, table, local.at[1]),
    ]
    for copy in loads:
        copy.start()

    barrier = pltpu.get_barrier_semaphore()
    peers = [
        (sec_up, f, t), (sec_dn, f, t), (sec_up, fpar, t), (sec_dn, fpar, t), (s, fpar, t), (s, zat(xh, 1), t), (s, zat(xh, -1), t),
        (s, f, ydev(1)), (s, f, ydev(2)), (s, f, ydev(3)),
    ]
    for where in peers:
        pl.semaphore_signal(barrier, inc=1, device_id=where, device_id_type=MESH)
    pl.semaphore_wait(barrier, len(peers))

    def put(src, dst, slot, where):
        remote(src, dst, raw_s.at[0], raw_r.at[slot], where).start()

    for side, section in ((0, sec_up), (1, sec_dn)):
        for away, other in ((0, f), (1, fpar)):
            dst = raw_e.at[2 * away + side]
            put(wkv_hbm, dst.at[:, pl.ds(0, 256)], 2 * away + side, (section, other, t))
            put(wq_hbm.at[:, pl.ds(0, 256)], dst.at[:, pl.ds(256, 256)], 2 * away + side, (section, other, t))
    for side, section in ((0, sec_up), (1, sec_dn)):
        put(wq_hbm.at[:, pl.ds(256, 768)], raw_l.at[side], 4 + side, (section, f, t))

    yin = []
    for j in (1, 3, 2):
        remote(e_hbm, ent.at[t], ya_s.at[0], ya_r.at[j - 1], (s, f, ydev(j))).start()
        src = lax.rem(t + YN - j, YN)
        yin.append(remote(e_hbm, ent.at[src], ya_s.at[0], ya_r.at[j - 1], (s, f, ydev(j))))
    for side, section in ((0, sec_up), (1, sec_dn)):
        put(wo_hbm, raw_o.at[side], 6 + side, (section, f, t))

    def mix(lo, hi):
        return (BEFORE_SHARE * lo.astype(jnp.float32) + AFTER_SHARE * hi.astype(jnp.float32)).astype(jnp.bfloat16)

    streams = (
        (ge, xh, None, 0, ROWS), (gl, xh, 0, 0, ROWS), (ge, xo, None, 0, ROWS),
        (oe, xh, None, 0, ROWS), (ol, xh, 1, 0, HALF), (oe, xo, None, 0, ROWS), (ol, xh, 1, HALF, HALF),
    )

    def zcopy(i, b, r, d):
        buf, _, _, row, rows = streams[i]
        block = buf.at[b, pl.ds(row, rows)]
        return remote(block, block, zs.at[i], zr.at[i, r], (s, zat(xh, d), t))

    def zslot(d, k):
        return k - 1 if d == 1 else 6 + k

    def zsend(i, d, k):
        zcopy(i, zat(streams[i][1], -d * (k - 1)), zslot(d, k), d).start()

    sign = 1 - 2 * core

    def xsend(i, off, slot):
        buf, _, late, row, rows = streams[i]
        block = buf.at[zat(xh, off), pl.ds(row, rows)]
        remote(block, block, xs.at[late], xr.at[late, slot], (s, fpar, t)).start()

    def xwait(late, slot):
        buf = (gl, ol)[late]
        both = buf.at[pl.ds(0, 2 if 0 < slot < 8 else 1)]
        remote(both, both, xs.at[late], xr.at[late, slot], (s, fpar, t)).wait_recv()

    def forward(i, k):
        x, late = streams[i][1:3]
        if k == 8:
            zcopy(i, zat(x, 8), 14, sign).wait_recv()
            if late is not None:
                xsend(i, 8, 8)
            return
        for d in (1, -1):
            zcopy(i, zat(x, -d * k), zslot(d, k), d).wait_recv()
            if k < 7:
                zsend(i, d, k + 1)
            if late is not None:
                xsend(i, -d * k, k)
        if k == 7:
            zcopy(i, zat(x, -7 * sign), 14, sign).start()

    def pair_of(k):
        far = lax.rem(z + k, 2)
        return lax.rem((z + 2 * ZN + far * (k - 1) - (1 - far) * k) // 2, ZN // 2)

    def arrived(dst, slot):
        remote(dst, dst, raw_s.at[0], raw_r.at[slot], (s, fpar, t)).wait_recv()

    for away, stream in ((0, 0), (1, 2)):
        arrived(raw_e.at[2 * away], 2 * away)
        arrived(raw_e.at[2 * away + 1], 2 * away + 1)
        ge[pl.ds((f, fpar)[away], 1)] = mix(raw_e[2 * away], raw_e[2 * away + 1])[None]
        zsend(stream, 1, 1)
        zsend(stream, -1, 1)
    for side in (0, 1):
        arrived(raw_l.at[side], 4 + side)
    gl[pl.ds(f, 1)] = mix(raw_l[0], raw_l[1])[None]
    zsend(1, 1, 1)
    zsend(1, -1, 1)
    xsend(1, 0, 0)
    for side in (0, 1):
        arrived(raw_o.at[side], 6 + side)
    oe[pl.ds(f, 1)] = mix(raw_o[0, :, 0:OE], raw_o[1, :, 0:OE])[None]
    ol[pl.ds(f, 1)] = mix(raw_o[0, :, OE:], raw_o[1, :, OE:])[None]
    early_o = remote(oe.at[f], oe.at[f], xe_s.at[0], xe_r.at[0], (s, fpar, t))
    early_o.start()

    def normalise():
        @pl.loop(0, 4)
        def _(m):
            rows = pl.ds(pl.multiple_of(m * 128, 128), 128)
            total = jnp.zeros((128, 1), jnp.float32)
            for c in range(YN):
                block = ent[c, rows, :].astype(jnp.float32)
                total = total + jnp.sum(block * block, axis=1, keepdims=True)
            factor = lax.rsqrt(total * (1.0 / (YN * FEAT)) + EPSILON)
            for c in range(YN):
                value = (ent[c, rows, :].astype(jnp.float32) * factor).astype(jnp.bfloat16)
                for i in range(4):
                    nrm[4 * c + i, rows, :] = value[:, 128 * i : 128 * i + 128]

    def accumulate(k, buf, base, width):
        pair = pair_of(k)

        @pl.loop(0, 2)
        def _(m):
            rows = pl.ds(pl.multiple_of(m * 256, 256), 256)
            left = jnp.concatenate([nrm[xh * 8 + pair, rows, :], nrm[xo * 8 + pair, rows, :]], axis=1)
            for col in range(0, width, 256):
                weight = jnp.concatenate(
                    [
                        buf[pl.ds(xh * ZN + 2 * pair, 2), :, col : col + 256].reshape(128, 256),
                        buf[pl.ds(xo * ZN + 2 * pair, 2), :, col : col + 256].reshape(128, 256),
                    ],
                    axis=0,
                )
                value = jnp.dot(left, weight, preferred_element_type=jnp.float32)
                at = slice(base + col, base + col + 256)
                if k > 1:
                    value = value + acc[rows, at]
                acc[rows, at] = value

    def accumulate_late(k):
        if k == 1:
            xwait(0, 0)
        xwait(0, k)
        accumulate(k, gl, QE, QL)

    def rotate(vectors, rows):
        meansq = jnp.mean(vectors * vectors, axis=-1, keepdims=True)
        normed = vectors * lax.rsqrt(meansq + EPSILON)
        turned = normed * table[0, rows, :] + pltpu.roll(normed, 64, 1) * table[1, rows, :]
        return turned.astype(jnp.bfloat16)

    def halves(step):
        @pl.loop(0, 4)
        def _(m):
            step(pl.ds(pl.multiple_of(m * 128, 128), 128))

    def finish_early(rows):
        ks[rows, :] = rotate(acc[rows, 0:128], rows)
        vs[rows, :] = acc[rows, 128:256].astype(jnp.bfloat16)
        qs[0, rows, :] = rotate(acc[rows, 256:384], rows)
        qs[1, rows, :] = rotate(acc[rows, 384:512], rows)

    def finish_late(rows):
        for h in range(2, 8):
            qs[h, rows, :] = rotate(acc[rows, QE + 128 * (h - 2) : QE + 128 * (h - 1)], rows)

    mul = LOG2E / math.sqrt(HEAD_DIM)
    sub = LOG2E * math.sqrt(HEAD_DIM)

    def expo(queries, keys, masked):
        scores = lax.dot_general(queries, keys, NT, preferred_element_type=jnp.float32)
        value = jnp.exp2(scores * mul - sub)
        if masked:
            row = lax.broadcasted_iota(jnp.int32, value.shape, 0)
            col = lax.broadcasted_iota(jnp.int32, value.shape, 1)
            value = jnp.where(row >= col, value, 0.0)
        return value

    def attend(h):
        cols = pl.ds(pl.multiple_of(h * 128, 128), 128)
        e = expo(qs[h, 0:256, :], ks[0:256, :], True)
        w = (e * (1.0 / jnp.sum(e, axis=-1, keepdims=True))).astype(jnp.bfloat16)
        mx[0:256, cols] = jnp.dot(w, vs[0:256, :], preferred_element_type=jnp.float32).astype(jnp.bfloat16)
        queries = qs[h, 256:512, :]
        e0 = expo(queries, ks[0:256, :], False)
        e1 = expo(queries, ks[256:512, :], True)
        r = 1.0 / (jnp.sum(e0, axis=-1, keepdims=True) + jnp.sum(e1, axis=-1, keepdims=True))
        w0 = (e0 * r).astype(jnp.bfloat16)
        w1 = (e1 * r).astype(jnp.bfloat16)
        mixed = jnp.dot(w0, vs[0:256, :], preferred_element_type=jnp.float32)
        mixed = mixed + jnp.dot(w1, vs[256:512, :], preferred_element_type=jnp.float32)
        mx[256:512, cols] = mixed.astype(jnp.bfloat16)

    def to_owner(k, slot, quarter, owner):
        j = lax.rem(owner + YN - t, YN) - 1
        remote(pb.at[slot], rb.at[j, quarter], ps.at[0], pr.at[j, quarter], (s, f, owner)).start()

    def partial(k):
        if k == 1:
            xwait(1, 0)
        xwait(1, k)
        pair = pair_of(k)
        quarter = lax.rem(pair, 4)

        @pl.loop(0, 2)
        def _(x):
            owner = 2 * x + pair // 4
            b = pl.ds(x * ZN + 2 * pair, 2)
            slot = 2 * (k - 1) + x
            first = oe[b].reshape(128, OE)
            second = ol[b].reshape(128, OL)
            value = lax.dot_general(mx[:, 0:OE], first, NT, preferred_element_type=jnp.float32)
            value = value + lax.dot_general(mx[:, OE:], second, NT, preferred_element_type=jnp.float32)
            value = value.astype(jnp.bfloat16)

            @pl.when(owner == t)
            def _():
                po[pl.ds(quarter, 1)] = value[None]

            @pl.when(owner != t)
            def _():
                pb[pl.ds(slot, 1)] = value[None]
                if k == 8:
                    to_owner(k, slot, quarter, owner)

            if k < 8:
                @pl.when(owner == ydev(2))
                def _():
                    for side in (0, 1):
                        half = pb.at[slot, pl.ds(256 * side, 256)]
                        remote(half, rl.at[k - 1, side], ps.at[0], rr.at[k - 1, side], (s, f, ydev(1 + 2 * side))).start()

    def relay(k):
        pair = pair_of(k)

        @pl.when(pair // 4 != lax.rem(t, 2))
        def _():
            for side in (0, 1):
                owner = ydev(1 + 2 * side)
                slot = 2 * (k - 1) + owner // 2
                dst = rl.at[k - 1, side]
                remote(dst, dst, ps.at[0], rr.at[k - 1, side], (s, f, owner)).wait_recv()
                rows = slice(256 * side, 256 * side + 256)
                total = pb[slot, rows, :].astype(jnp.float32) + rl[k - 1, side].astype(jnp.float32)
                pb[pl.ds(slot, 1), rows, :] = total.astype(jnp.bfloat16)[None]
                to_owner(k, slot, lax.rem(pair, 4), owner)

    for k in range(1, 8):
        for i in (0, 2):
            forward(i, k)
        if k > 4:
            accumulate(EARLY[k][0], ge, 0, QE)
        forward(1, k)
        if k == 7:
            early_o.wait_recv()
            for i in (3, 4, 6, 5):
                zsend(i, 1, 1)
                zsend(i, -1, 1)
            xsend(4, 0, 0)
            xsend(6, 0, 0)
        if k == 4:
            loads[0].wait()
            for copy in yin:
                copy.wait_recv()
            normalise()
            accumulate(1, ge, 0, QE)
            accumulate_late(1)
        if k > 4:
            accumulate_late(EARLY[k][0])
            for i in EARLY[k][1:]:
                accumulate(i, ge, 0, QE)
                accumulate_late(i)

    forward(0, 8)
    forward(2, 8)
    accumulate(7, ge, 0, QE)
    forward(1, 8)
    forward(3, 1)
    accumulate_late(7)
    accumulate(8, ge, 0, QE)
    loads[1].wait()
    halves(finish_early)
    forward(4, 1)
    forward(6, 1)
    attend(0)
    forward(5, 1)
    attend(1)
    forward(3, 2)
    accumulate_late(8)
    halves(finish_late)
    forward(4, 2)
    forward(6, 2)
    attend(2)
    forward(5, 2)
    attend(3)
    forward(3, 3)
    attend(4)
    attend(5)
    forward(4, 3)
    attend(6)
    forward(6, 3)
    forward(5, 3)
    attend(7)
    forward(3, 4)
    partial(1)
    forward(4, 4)
    forward(6, 4)
    forward(5, 4)
    partial(2)
    for k in range(5, 9):
        forward(3, k)
        forward(4, k)
        relay(k - 4)
        forward(6, k)
        forward(5, k)
        partial(k - 2)
    relay(5)
    partial(7)
    relay(6)
    partial(8)
    relay(7)

    for k in range(1, 9):
        pair = pair_of(k)
        quarter = lax.rem(pair, 4)

        @pl.when(pair // 4 == lax.rem(t, 2))
        def _():
            sources = (0, 2) if k < 8 else (0, 2, 1)
            for j in sources:
                dst = rb.at[j, quarter]
                remote(dst, dst, ps.at[0], pr.at[j, quarter], (s, f, ydev(1))).wait_recv()
            cols = pl.ds(pl.multiple_of(quarter * 128, 128), 128)
            total = po[quarter].astype(jnp.float32)
            for j in sources:
                total = total + rb[j, quarter].astype(jnp.float32)
            out_ref[:, cols] = (ent[t, :, cols].astype(jnp.float32) + total).astype(jnp.bfloat16)

    def left(ref, sem):
        remote(ref, ref, sem, raw_r.at[0], (s, fpar, t)).wait_send()

    left(ge.at[pl.ds(0, 11)], raw_s.at[0])
    left(ent.at[pl.ds(0, 3)], ya_s.at[0])
    early_o.wait_send()
    for i, (buf, _, _, row, rows) in enumerate(streams):
        left(buf.at[pl.ds(0, 15), pl.ds(row, rows)], zs.at[i])
    for late, buf in enumerate((gl, ol)):
        left(buf.at[pl.ds(0, 16)], xs.at[late])
    left(pb.at[pl.ds(0, 12)], ps.at[0])


def body(entering, w_query, w_keyval, w_out):
    bf16, f32, vmem, dma = jnp.bfloat16, jnp.float32, pltpu.VMEM, pltpu.SemaphoreType.DMA
    operands = (
        entering[0], w_query[0], w_keyval.reshape(ROWS, 256), jnp.swapaxes(w_out[0], 0, 1), jnp.asarray(rope_tables())
    )
    out = pl.pallas_call(
        kernel,
        out_shape=jax.ShapeDtypeStruct((SEQ, FEAT), bf16),
        in_specs=[pl.BlockSpec(memory_space=pl.ANY)] * len(operands),
        out_specs=pl.BlockSpec(memory_space=vmem),
        scratch_shapes=[
            vmem((YN, SEQ, FEAT), bf16), vmem((16, SEQ, 128), bf16), vmem((2, SEQ, HEAD_DIM), f32),
            vmem((4, ROWS, QE), bf16), vmem((2, ROWS, QL), bf16), vmem((2, ROWS, OE + OL), bf16),
            vmem((2 * ZN, ROWS, QE), bf16), vmem((2 * ZN, ROWS, QL), bf16),
            vmem((2 * ZN, ROWS, OE), bf16), vmem((2 * ZN, ROWS, OL), bf16),
            vmem((SEQ, QE + QL), f32),
            vmem((8, SEQ, HEAD_DIM), bf16), vmem((SEQ, HEAD_DIM), bf16), vmem((SEQ, HEAD_DIM), bf16),
            vmem((SEQ, OE + OL), bf16), vmem((16, SEQ, 128), bf16), vmem((4, SEQ, 128), bf16),
            vmem((3, 4, SEQ, 128), bf16), vmem((7, 2, 256, 128), bf16),
            dma((2,)), dma((1,)), dma((8,)), dma((1,)), dma((3,)), dma((7,)), dma((7, 15)),
            dma((2,)), dma((2, 9)), dma((1,)), dma((1,)), dma((1,)), dma((3, 4)), dma((7, 2)),
        ],
        compiler_params=pltpu.CompilerParams(
            collective_id=0, has_side_effects=True, vmem_limit_bytes=40 * 1024 * 1024
        ),
        name="section",
    )(*(pltpu.with_memory_space_constraint(value, pltpu.HBM) for value in operands))
    return out[None]


def solution(mesh):
    in_specs = (
        P("section", "fsdp", "tensor"),
        P("section", "fsdp", "tensor"),
        P("section", "fsdp", "tensor", None),
        P("section", "tensor", "fsdp"),
    )
    out_specs = P("section", "fsdp", "tensor")
    return jax.shard_map(body, mesh=mesh, in_specs=in_specs, out_specs=out_specs, check_vma=False)
```

```python
import math

import jax
import jax.numpy as jnp
import numpy as np
from jax import lax
from jax.experimental import pallas as pl
from jax.experimental.pallas import tpu as pltpu
from jax.sharding import PartitionSpec as P

HEAD_DIM = 128
EPSILON = 1e-06
ROPE_BASE = 1000000.0
BEFORE_SHARE = 0.6
AFTER_SHARE = 0.4
MESH = pl.DeviceIdType.MESH
RECV = (0, 1, 2, 0, 1, 2, 3)

ZN = 16
SEC = 4
YN = 4
SEQ = 512
FEAT = 512
ROWS = 64
QE = 512
QL = 768
OE = 384
OL = 640
HALF = ROWS // 2
LOG2E = math.log2(math.e)
EARLY = {5: (2, 3), 6: (4, 5), 7: (6,)}
NT = (((1,), (1,)), ((), ()))


def rope_tables():
    half = HEAD_DIM // 2
    exponent = np.arange(half, dtype=np.float64) * (2.0 / HEAD_DIM)
    angles = np.arange(SEQ, dtype=np.float64)[:, None] * np.exp(-exponent * math.log(ROPE_BASE))[None, :]
    cosine, sine = np.cos(angles), np.sin(angles)
    tables = np.concatenate([cosine, cosine], axis=1), np.concatenate([-sine, sine], axis=1)
    return np.stack(tables).astype(np.float32)


def kernel(
    e_hbm, wq_hbm, wkv_hbm, wo_hbm, table_hbm, out_ref,
    ent, nrm, table, raw_e, raw_l, raw_o,
    ge, gl, oe, ol, acc, qs, ks, vs, mx, pb, po, rb, rl,
    local, raw_s, raw_r, ya_s, ya_r, zs, zr, xs, xr, xe_s, xe_r, ps, pr, rr,
):
    s, f, t = lax.axis_index("section"), lax.axis_index("fsdp"), lax.axis_index("tensor")
    core = lax.rem(s, 2)
    xh = f // ZN
    z = lax.rem(f, ZN)
    xo = 1 - xh
    fpar = xo * ZN + z
    sec_up, sec_dn = lax.rem(s + 1, SEC), lax.rem(s + SEC - 1, SEC)

    def ydev(j):
        return lax.rem(t + j, YN)

    def zat(x, off):
        return x * ZN + lax.rem(z + 2 * ZN + off, ZN)

    def remote(src, dst, ss, rs, where):
        return pltpu.make_async_remote_copy(
            src_ref=src, dst_ref=dst, send_sem=ss, recv_sem=rs, device_id=where, device_id_type=MESH
        )

    loads = [
        pltpu.make_async_copy(e_hbm, ent.at[t], local.at[0]),
        pltpu.make_async_copy(table_hbm, table, local.at[1]),
    ]
    for copy in loads:
        copy.start()

    barrier = pltpu.get_barrier_semaphore()
    peers = [
        (sec_up, f, t), (sec_dn, f, t), (sec_up, fpar, t), (sec_dn, fpar, t), (s, fpar, t), (s, zat(xh, 1), t), (s, zat(xh, -1), t),
        (s, f, ydev(1)), (s, f, ydev(2)), (s, f, ydev(3)),
    ]
    for where in peers:
        pl.semaphore_signal(barrier, inc=1, device_id=where, device_id_type=MESH)
    pl.semaphore_wait(barrier, len(peers))

    def put(src, dst, slot, where):
        remote(src, dst, raw_s.at[0], raw_r.at[slot], where).start()

    for away, other in ((0, f), (1, fpar)):
        for side, section in ((0, sec_up), (1, sec_dn)):
            dst = raw_e.at[2 * away + side]
            put(wkv_hbm, dst.at[:, pl.ds(0, 256)], 2 * away + side, (section, other, t))
            put(wq_hbm.at[:, pl.ds(0, 256)], dst.at[:, pl.ds(256, 256)], 2 * away + side, (section, other, t))
    for side, section in ((0, sec_up), (1, sec_dn)):
        put(wq_hbm.at[:, pl.ds(256, 768)], raw_l.at[side], 4 + side, (section, f, t))

    yin = []
    for j in (1, 3, 2):
        remote(e_hbm, ent.at[t], ya_s.at[0], ya_r.at[j - 1], (s, f, ydev(j))).start()
        src = lax.rem(t + YN - j, YN)
        yin.append(remote(e_hbm, ent.at[src], ya_s.at[0], ya_r.at[j - 1], (s, f, ydev(j))))
    for side, section in ((0, sec_up), (1, sec_dn)):
        put(wo_hbm, raw_o.at[side], 6 + side, (section, f, t))

    def mix(lo, hi):
        return (BEFORE_SHARE * lo.astype(jnp.float32) + AFTER_SHARE * hi.astype(jnp.float32)).astype(jnp.bfloat16)

    streams = (
        (ge, xh, None, 0, ROWS), (gl, xh, 0, 0, ROWS), (ge, xo, None, 0, ROWS),
        (oe, xh, None, 0, ROWS), (ol, xh, 1, 0, HALF), (oe, xo, None, 0, ROWS), (ol, xh, 1, HALF, HALF),
    )

    def zcopy(i, b, r, d):
        buf, _, _, row, rows = streams[i]
        block = buf.at[b, pl.ds(row, rows)]
        return remote(block, block, zs.at[i], zr.at[RECV[i], r], (s, zat(xh, d), t))

    def zslot(d, k):
        return k - 1 if d == 1 else 6 + k

    def zsend(i, d, k):
        zcopy(i, zat(streams[i][1], -d * (k - 1)), zslot(d, k), d).start()

    sign = 1 - 2 * core

    def xsend(i, off, slot):
        buf, _, late, row, rows = streams[i]
        block = buf.at[zat(xh, off), pl.ds(row, rows)]
        remote(block, block, xs.at[late], xr.at[late, slot], (s, fpar, t)).start()

    def xwait(late, slot):
        buf = (gl, ol)[late]
        both = buf.at[pl.ds(0, 2 if 0 < slot < 8 else 1)]
        remote(both, both, xs.at[late], xr.at[late, slot], (s, fpar, t)).wait_recv()

    def cross(i, k):
        for d in (1, -1):
            xsend(i, -d * k, k)

    def forward(i, k, crossing=True):
        x, late = streams[i][1:3]
        if k == 8:
            zcopy(i, zat(x, 8), 14, sign).wait_recv()
            if late is not None:
                xsend(i, 8, 8)
            return
        for d in (1, -1):
            zcopy(i, zat(x, -d * k), zslot(d, k), d).wait_recv()
            if k < 7:
                zsend(i, d, k + 1)
            if late is not None and crossing:
                xsend(i, -d * k, k)
        if k == 7:
            zcopy(i, zat(x, -7 * sign), 14, sign).start()

    def pair_of(k):
        far = lax.rem(z + k, 2)
        return lax.rem((z + 2 * ZN + far * (k - 1) - (1 - far) * k) // 2, ZN // 2)

    def arrived(dst, slot):
        remote(dst, dst, raw_s.at[0], raw_r.at[slot], (s, fpar, t)).wait_recv()

    for away, stream in ((0, 0), (1, 2)):
        arrived(raw_e.at[2 * away], 2 * away)
        arrived(raw_e.at[2 * away + 1], 2 * away + 1)
        ge[pl.ds((f, fpar)[away], 1)] = mix(raw_e[2 * away], raw_e[2 * away + 1])[None]
        zsend(stream, 1, 1)
        zsend(stream, -1, 1)
    for side in (0, 1):
        arrived(raw_l.at[side], 4 + side)
    gl[pl.ds(f, 1)] = mix(raw_l[0], raw_l[1])[None]
    zsend(1, 1, 1)
    zsend(1, -1, 1)
    xsend(1, 0, 0)
    for side in (0, 1):
        arrived(raw_o.at[side], 6 + side)
    oe[pl.ds(f, 1)] = mix(raw_o[0, :, 0:OE], raw_o[1, :, 0:OE])[None]
    ol[pl.ds(f, 1)] = mix(raw_o[0, :, OE:], raw_o[1, :, OE:])[None]
    early_o = remote(oe.at[f], oe.at[f], xe_s.at[0], xe_r.at[0], (s, fpar, t))
    early_o.start()

    def normalise():
        @pl.loop(0, 4)
        def _(m):
            rows = pl.ds(pl.multiple_of(m * 128, 128), 128)
            total = jnp.zeros((128, 1), jnp.float32)
            for c in range(YN):
                block = ent[c, rows, :].astype(jnp.float32)
                total = total + jnp.sum(block * block, axis=1, keepdims=True)
            factor = lax.rsqrt(total * (1.0 / (YN * FEAT)) + EPSILON)
            for c in range(YN):
                value = (ent[c, rows, :].astype(jnp.float32) * factor).astype(jnp.bfloat16)
                for i in range(4):
                    nrm[4 * c + i, rows, :] = value[:, 128 * i : 128 * i + 128]

    def accumulate(k, buf, base, width):
        pair = pair_of(k)

        @pl.loop(0, 2)
        def _(m):
            rows = pl.ds(pl.multiple_of(m * 256, 256), 256)
            left = jnp.concatenate([nrm[xh * 8 + pair, rows, :], nrm[xo * 8 + pair, rows, :]], axis=1)
            for col in range(0, width, 256):
                weight = jnp.concatenate(
                    [
                        buf[pl.ds(xh * ZN + 2 * pair, 2), :, col : col + 256].reshape(128, 256),
                        buf[pl.ds(xo * ZN + 2 * pair, 2), :, col : col + 256].reshape(128, 256),
                    ],
                    axis=0,
                )
                value = jnp.dot(left, weight, preferred_element_type=jnp.float32)
                at = slice(base + col, base + col + 256)
                if k > 1:
                    value = value + acc[rows, at]
                acc[rows, at] = value

    def accumulate_late(k):
        if k == 1:
            xwait(0, 0)
        xwait(0, k)
        accumulate(k, gl, QE, QL)

    def rotate(vectors, rows):
        meansq = jnp.mean(vectors * vectors, axis=-1, keepdims=True)
        normed = vectors * lax.rsqrt(meansq + EPSILON)
        turned = normed * table[0, rows, :] + pltpu.roll(normed, 64, 1) * table[1, rows, :]
        return turned.astype(jnp.bfloat16)

    def halves(step):
        @pl.loop(0, 4)
        def _(m):
            step(pl.ds(pl.multiple_of(m * 128, 128), 128))

    def finish_early(rows):
        ks[rows, :] = rotate(acc[rows, 0:128], rows)
        vs[rows, :] = acc[rows, 128:256].astype(jnp.bfloat16)
        qs[0, rows, :] = rotate(acc[rows, 256:384], rows)
        qs[1, rows, :] = rotate(acc[rows, 384:512], rows)

    def finish_late(heads):
        def step(rows):
            for h in heads:
                qs[h, rows, :] = rotate(acc[rows, QE + 128 * (h - 2) : QE + 128 * (h - 1)], rows)

        halves(step)

    mul = LOG2E / math.sqrt(HEAD_DIM)
    sub = LOG2E * math.sqrt(HEAD_DIM)

    def expo(queries, keys, masked):
        scores = lax.dot_general(queries, keys, NT, preferred_element_type=jnp.float32)
        value = jnp.exp2(scores * mul - sub)
        if masked:
            row = lax.broadcasted_iota(jnp.int32, value.shape, 0)
            col = lax.broadcasted_iota(jnp.int32, value.shape, 1)
            value = jnp.where(row >= col, value, 0.0)
        return value

    def attend(h):
        cols = slice(h * 128, h * 128 + 128)
        e = expo(qs[h, 0:256, :], ks[0:256, :], True)
        mixed = jnp.dot(e.astype(jnp.bfloat16), vs[0:256, :], preferred_element_type=jnp.float32)
        mx[0:256, cols] = (mixed * (1.0 / jnp.sum(e, axis=-1, keepdims=True))).astype(jnp.bfloat16)
        queries = qs[h, 256:512, :]
        e0 = expo(queries, ks[0:256, :], False)
        e1 = expo(queries, ks[256:512, :], True)
        mixed = jnp.dot(e0.astype(jnp.bfloat16), vs[0:256, :], preferred_element_type=jnp.float32)
        mixed = mixed + jnp.dot(e1.astype(jnp.bfloat16), vs[256:512, :], preferred_element_type=jnp.float32)
        r = 1.0 / (jnp.sum(e0, axis=-1, keepdims=True) + jnp.sum(e1, axis=-1, keepdims=True))
        mx[256:512, cols] = (mixed * r).astype(jnp.bfloat16)

    def to_owner(k, slot, quarter, owner):
        j = lax.rem(owner + YN - t, YN) - 1
        remote(pb.at[slot], rb.at[j, quarter], ps.at[0], pr.at[j, quarter], (s, f, owner)).start()

    def partial(k):
        if k == 1:
            xwait(1, 0)
        xwait(1, k)
        pair = pair_of(k)
        quarter = lax.rem(pair, 4)

        def weights(buf, width):
            return jnp.concatenate([buf[pl.ds(x * ZN + 2 * pair, 2)].reshape(128, width) for x in (0, 1)], axis=0)

        both = lax.dot_general(mx[:, 0:OE], weights(oe, OE), NT, preferred_element_type=jnp.float32)
        both = both + lax.dot_general(mx[:, OE:], weights(ol, OL), NT, preferred_element_type=jnp.float32)
        both = both.astype(jnp.bfloat16)
        for x in (0, 1):
            owner = 2 * x + pair // 4
            slot = 2 * (k - 1) + x
            value = both[:, 128 * x : 128 * x + 128]

            @pl.when(owner == t)
            def _():
                po[pl.ds(quarter, 1)] = value[None]

            @pl.when(owner != t)
            def _():
                pb[slot] = value
                if k == 8:
                    to_owner(k, slot, quarter, owner)

            if k < 8:
                @pl.when(owner == ydev(2))
                def _():
                    for side in (0, 1):
                        half = pb.at[slot, pl.ds(256 * side, 256)]
                        remote(half, rl.at[k - 1, side], ps.at[0], rr.at[k - 1, side], (s, f, ydev(1 + 2 * side))).start()

    def relay(k):
        pair = pair_of(k)

        @pl.when(pair // 4 != lax.rem(t, 2))
        def _():
            for side in (0, 1):
                owner = ydev(1 + 2 * side)
                slot = 2 * (k - 1) + owner // 2
                dst = rl.at[k - 1, side]
                remote(dst, dst, ps.at[0], rr.at[k - 1, side], (s, f, owner)).wait_recv()
                rows = slice(256 * side, 256 * side + 256)
                total = pb[slot, rows, :].astype(jnp.float32) + rl[k - 1, side].astype(jnp.float32)
                pb[pl.ds(slot, 1), rows, :] = total.astype(jnp.bfloat16)[None]
                to_owner(k, slot, lax.rem(pair, 4), owner)

    for k in range(1, 8):
        for i in (0, 2):
            forward(i, k)
        if k > 4:
            accumulate(EARLY[k][0], ge, 0, QE)
        forward(1, k)
        if k == 6:
            early_o.wait_recv()
            for i in (3, 4, 6, 5):
                zsend(i, 1, 1)
                zsend(i, -1, 1)
        if k == 4:
            loads[0].wait()
            for copy in yin:
                copy.wait_recv()
            normalise()
            accumulate(1, ge, 0, QE)
            accumulate_late(1)
        if k > 4:
            accumulate_late(EARLY[k][0])
            for i in EARLY[k][1:]:
                accumulate(i, ge, 0, QE)
                accumulate_late(i)

    forward(3, 1)
    forward(4, 1, crossing=False)
    forward(6, 1, crossing=False)
    forward(0, 8)
    forward(5, 1)
    forward(2, 8)
    accumulate(7, ge, 0, QE)
    forward(1, 8)
    for i in (4, 6):
        xsend(i, 0, 0)
        cross(i, 1)
    accumulate(8, ge, 0, QE)
    loads[1].wait()
    halves(finish_early)
    accumulate_late(7)
    attend(0)
    forward(3, 2)
    attend(1)
    forward(4, 2)
    forward(6, 2)
    forward(5, 2)
    accumulate_late(8)
    finish_late((2, 3, 4))
    forward(3, 3)
    attend(2)
    forward(4, 3)
    finish_late((5, 6, 7))
    forward(6, 3)
    forward(5, 3)
    attend(3)
    attend(4)
    forward(3, 4)
    attend(5)
    forward(4, 4)
    attend(6)
    forward(6, 4)
    attend(7)
    forward(5, 4)
    partial(1)
    forward(3, 5)
    partial(2)
    forward(4, 5)
    forward(6, 5)
    forward(5, 5)
    forward(3, 6)
    partial(3)
    forward(4, 6)
    relay(1)
    forward(6, 6)
    relay(2)
    forward(5, 6)
    partial(4)
    for k in (7, 8):
        forward(4, k)
        partial(k - 2)
        forward(6, k)
        relay(k - 4)
        forward(3, k)
        forward(5, k)
    relay(5)
    partial(7)
    relay(6)
    partial(8)
    relay(7)

    for k in range(1, 9):
        pair = pair_of(k)
        quarter = lax.rem(pair, 4)

        @pl.when(pair // 4 == lax.rem(t, 2))
        def _():
            sources = (0, 2) if k < 8 else (0, 2, 1)
            for j in sources:
                dst = rb.at[j, quarter]
                remote(dst, dst, ps.at[0], pr.at[j, quarter], (s, f, ydev(1))).wait_recv()
            cols = pl.ds(pl.multiple_of(quarter * 128, 128), 128)
            total = po[quarter].astype(jnp.float32)
            for j in sources:
                total = total + rb[j, quarter].astype(jnp.float32)
            out_ref[:, cols] = (ent[t, :, cols].astype(jnp.float32) + total).astype(jnp.bfloat16)

    def left(ref, sem):
        remote(ref, ref, sem, raw_r.at[0], (s, fpar, t)).wait_send()

    left(ge.at[pl.ds(0, 11)], raw_s.at[0])
    left(ent.at[pl.ds(0, 3)], ya_s.at[0])
    early_o.wait_send()
    for i, (buf, _, _, row, rows) in enumerate(streams):
        left(buf.at[pl.ds(0, 15), pl.ds(row, rows)], zs.at[i])
    for late, buf in enumerate((gl, ol)):
        left(buf.at[pl.ds(0, 16)], xs.at[late])
    left(pb.at[pl.ds(0, 12)], ps.at[0])


def body(entering, w_query, w_keyval, w_out):
    bf16, f32, vmem, dma = jnp.bfloat16, jnp.float32, pltpu.VMEM, pltpu.SemaphoreType.DMA
    operands = (
        entering[0], w_query[0], w_keyval.reshape(ROWS, 256), jnp.swapaxes(w_out[0], 0, 1), jnp.asarray(rope_tables())
    )
    out = pl.pallas_call(
        kernel,
        out_shape=jax.ShapeDtypeStruct((SEQ, FEAT), bf16),
        in_specs=[pl.BlockSpec(memory_space=pl.ANY)] * len(operands),
        out_specs=pl.BlockSpec(memory_space=vmem),
        scratch_shapes=[
            vmem((YN, SEQ, FEAT), bf16), vmem((16, SEQ, 128), bf16), vmem((2, SEQ, HEAD_DIM), f32),
            vmem((4, ROWS, QE), bf16), vmem((2, ROWS, QL), bf16), vmem((2, ROWS, OE + OL), bf16),
            vmem((2 * ZN, ROWS, QE), bf16), vmem((2 * ZN, ROWS, QL), bf16),
            vmem((2 * ZN, ROWS, OE), bf16), vmem((2 * ZN, ROWS, OL), bf16),
            vmem((SEQ, QE + QL), f32),
            vmem((8, SEQ, HEAD_DIM), bf16), vmem((SEQ, HEAD_DIM), bf16), vmem((SEQ, HEAD_DIM), bf16),
            vmem((SEQ, OE + OL), bf16), vmem((16, SEQ, 128), bf16), vmem((4, SEQ, 128), bf16),
            vmem((3, 4, SEQ, 128), bf16), vmem((7, 2, 256, 128), bf16),
            dma((2,)), dma((1,)), dma((8,)), dma((1,)), dma((3,)), dma((7,)), dma((4, 15)),
            dma((2,)), dma((2, 9)), dma((1,)), dma((1,)), dma((1,)), dma((3, 4)), dma((7, 2)),
        ],
        compiler_params=pltpu.CompilerParams(
            collective_id=0, has_side_effects=True, vmem_limit_bytes=40 * 1024 * 1024
        ),
        name="section",
    )(*(pltpu.with_memory_space_constraint(value, pltpu.HBM) for value in operands))
    return out[None]


def solution(mesh):
    in_specs = (
        P("section", "fsdp", "tensor"),
        P("section", "fsdp", "tensor"),
        P("section", "fsdp", "tensor", None),
        P("section", "tensor", "fsdp"),
    )
    out_specs = P("section", "fsdp", "tensor")
    return jax.shard_map(body, mesh=mesh, in_specs=in_specs, out_specs=out_specs, check_vma=False)
```

```python
import math

import jax
import jax.numpy as jnp
import numpy as np
from jax import lax
from jax.experimental import pallas as pl
from jax.experimental.pallas import tpu as pltpu
from jax.sharding import PartitionSpec as P

HEAD_DIM = 128
EPSILON = 1e-06
ROPE_BASE = 1000000.0
BEFORE_SHARE = 0.6
AFTER_SHARE = 0.4
MESH = pl.DeviceIdType.MESH
RECV = (0, 1, 2, 0, 1, 2, 3)

ZN = 16
SEC = 4
YN = 4
SEQ = 512
FEAT = 512
ROWS = 64
QE = 512
QL = 768
OE = 384
OL = 640
HALF = ROWS // 2
LOG2E = math.log2(math.e)
EARLY = {5: (2, 3), 6: (4, 5), 7: (6,)}
NT = (((1,), (1,)), ((), ()))


def rope_tables():
    half = HEAD_DIM // 2
    exponent = np.arange(half, dtype=np.float64) * (2.0 / HEAD_DIM)
    angles = np.arange(SEQ, dtype=np.float64)[:, None] * np.exp(-exponent * math.log(ROPE_BASE))[None, :]
    cosine, sine = np.cos(angles), np.sin(angles)
    tables = np.concatenate([cosine, cosine], axis=1), np.concatenate([-sine, sine], axis=1)
    return np.stack(tables).astype(np.float32)


def kernel(
    e_hbm, wq_hbm, wkv_hbm, wo_hbm, table_hbm, out_ref,
    ent, nrm, table, raw_e, raw_l, raw_o,
    ge, gl, oe, ol, acc, qs, ks, vs, mx, pb, po, rb, rl,
    local, raw_s, raw_r, ya_s, ya_r, zs, zr, xs, xr, xe_s, xe_r, ps, pr, rr,
):
    s, f, t = lax.axis_index("section"), lax.axis_index("fsdp"), lax.axis_index("tensor")
    core = lax.rem(s, 2)
    xh = f // ZN
    z = lax.rem(f, ZN)
    xo = 1 - xh
    fpar = xo * ZN + z
    sec_up, sec_dn = lax.rem(s + 1, SEC), lax.rem(s + SEC - 1, SEC)

    def ydev(j):
        return lax.rem(t + j, YN)

    def zat(x, off):
        return x * ZN + lax.rem(z + 2 * ZN + off, ZN)

    def remote(src, dst, ss, rs, where):
        return pltpu.make_async_remote_copy(
            src_ref=src, dst_ref=dst, send_sem=ss, recv_sem=rs, device_id=where, device_id_type=MESH
        )

    loads = [
        pltpu.make_async_copy(e_hbm, ent.at[t], local.at[0]),
        pltpu.make_async_copy(table_hbm, table, local.at[1]),
    ]
    for copy in loads:
        copy.start()

    barrier = pltpu.get_barrier_semaphore()
    peers = [
        (sec_up, f, t), (sec_dn, f, t), (sec_up, fpar, t), (sec_dn, fpar, t), (s, fpar, t), (s, zat(xh, 1), t), (s, zat(xh, -1), t),
        (s, f, ydev(1)), (s, f, ydev(2)), (s, f, ydev(3)),
    ]
    for where in peers:
        pl.semaphore_signal(barrier, inc=1, device_id=where, device_id_type=MESH)
    pl.semaphore_wait(barrier, len(peers))

    def put(src, dst, slot, where):
        remote(src, dst, raw_s.at[0], raw_r.at[slot], where).start()

    for away, other in ((0, f), (1, fpar)):
        for side, section in ((0, sec_up), (1, sec_dn)):
            dst = raw_e.at[2 * away + side]
            put(wkv_hbm, dst.at[:, pl.ds(0, 256)], 2 * away + side, (section, other, t))
            put(wq_hbm.at[:, pl.ds(0, 256)], dst.at[:, pl.ds(256, 256)], 2 * away + side, (section, other, t))
    for side, section in ((0, sec_up), (1, sec_dn)):
        put(wq_hbm.at[:, pl.ds(256, 768)], raw_l.at[side], 4 + side, (section, f, t))

    yin = []
    for j in (1, 3, 2):
        remote(e_hbm, ent.at[t], ya_s.at[0], ya_r.at[j - 1], (s, f, ydev(j))).start()
        src = lax.rem(t + YN - j, YN)
        yin.append(remote(e_hbm, ent.at[src], ya_s.at[0], ya_r.at[j - 1], (s, f, ydev(j))))
    for side, section in ((0, sec_up), (1, sec_dn)):
        put(wo_hbm, raw_o.at[side], 6 + side, (section, f, t))

    def mix(lo, hi):
        return (BEFORE_SHARE * lo.astype(jnp.float32) + AFTER_SHARE * hi.astype(jnp.float32)).astype(jnp.bfloat16)

    streams = (
        (ge, xh, None, 0, ROWS), (gl, xh, 0, 0, ROWS), (ge, xo, None, 0, ROWS),
        (oe, xh, None, 0, ROWS), (ol, xh, 1, 0, HALF), (oe, xo, None, 0, ROWS), (ol, xh, 1, HALF, HALF),
    )

    def zcopy(i, b, r, d):
        buf, _, _, row, rows = streams[i]
        block = buf.at[b, pl.ds(row, rows)]
        return remote(block, block, zs.at[i], zr.at[RECV[i], r], (s, zat(xh, d), t))

    def zslot(d, k):
        return k - 1 if d == 1 else 6 + k

    def zsend(i, d, k):
        zcopy(i, zat(streams[i][1], -d * (k - 1)), zslot(d, k), d).start()

    sign = 1 - 2 * core

    def xsend(i, off, slot):
        buf, _, late, row, rows = streams[i]
        block = buf.at[zat(xh, off), pl.ds(row, rows)]
        remote(block, block, xs.at[late], xr.at[late, slot], (s, fpar, t)).start()

    def xwait(late, slot):
        buf = (gl, ol)[late]
        both = buf.at[pl.ds(0, 2 if 0 < slot < 8 else 1)]
        remote(both, both, xs.at[late], xr.at[late, slot], (s, fpar, t)).wait_recv()

    def cross(i, k):
        for d in (1, -1):
            xsend(i, -d * k, k)

    def forward(i, k, crossing=True):
        x, late = streams[i][1:3]
        if k == 8:
            zcopy(i, zat(x, 8), 14, sign).wait_recv()
            if late is not None:
                xsend(i, 8, 8)
            return
        for d in (1, -1):
            zcopy(i, zat(x, -d * k), zslot(d, k), d).wait_recv()
            if k < 7:
                zsend(i, d, k + 1)
            if late is not None and crossing:
                xsend(i, -d * k, k)
        if k == 7:
            zcopy(i, zat(x, -7 * sign), 14, sign).start()

    def pair_of(k):
        far = lax.rem(z + k, 2)
        return lax.rem((z + 2 * ZN + far * (k - 1) - (1 - far) * k) // 2, ZN // 2)

    def arrived(dst, slot):
        remote(dst, dst, raw_s.at[0], raw_r.at[slot], (s, fpar, t)).wait_recv()

    for away, stream in ((0, 0), (1, 2)):
        arrived(raw_e.at[2 * away], 2 * away)
        arrived(raw_e.at[2 * away + 1], 2 * away + 1)
        ge[pl.ds((f, fpar)[away], 1)] = mix(raw_e[2 * away], raw_e[2 * away + 1])[None]
        zsend(stream, 1, 1)
        zsend(stream, -1, 1)
    for side in (0, 1):
        arrived(raw_l.at[side], 4 + side)
    gl[pl.ds(f, 1)] = mix(raw_l[0], raw_l[1])[None]
    zsend(1, 1, 1)
    zsend(1, -1, 1)
    xsend(1, 0, 0)
    for side in (0, 1):
        arrived(raw_o.at[side], 6 + side)
    oe[pl.ds(f, 1)] = mix(raw_o[0, :, 0:OE], raw_o[1, :, 0:OE])[None]
    ol[pl.ds(f, 1)] = mix(raw_o[0, :, OE:], raw_o[1, :, OE:])[None]
    early_o = remote(oe.at[f], oe.at[f], xe_s.at[0], xe_r.at[0], (s, fpar, t))
    early_o.start()

    def normalise():
        @pl.loop(0, 4)
        def _(m):
            rows = pl.ds(pl.multiple_of(m * 128, 128), 128)
            total = jnp.zeros((128, 1), jnp.float32)
            for c in range(YN):
                block = ent[c, rows, :].astype(jnp.float32)
                total = total + jnp.sum(block * block, axis=1, keepdims=True)
            factor = lax.rsqrt(total * (1.0 / (YN * FEAT)) + EPSILON)
            for c in range(YN):
                value = (ent[c, rows, :].astype(jnp.float32) * factor).astype(jnp.bfloat16)
                for i in range(4):
                    nrm[4 * c + i, rows, :] = value[:, 128 * i : 128 * i + 128]

    def accumulate(k, buf, base, width):
        pair = pair_of(k)

        @pl.loop(0, 2)
        def _(m):
            rows = pl.ds(pl.multiple_of(m * 256, 256), 256)
            left = jnp.concatenate([nrm[xh * 8 + pair, rows, :], nrm[xo * 8 + pair, rows, :]], axis=1)
            for col in range(0, width, 256):
                weight = jnp.concatenate(
                    [
                        buf[pl.ds(xh * ZN + 2 * pair, 2), :, col : col + 256].reshape(128, 256),
                        buf[pl.ds(xo * ZN + 2 * pair, 2), :, col : col + 256].reshape(128, 256),
                    ],
                    axis=0,
                )
                value = jnp.dot(left, weight, preferred_element_type=jnp.float32)
                at = slice(base + col, base + col + 256)
                if k > 1:
                    value = value + acc[rows, at]
                acc[rows, at] = value

    def accumulate_late(k):
        if k == 1:
            xwait(0, 0)
        xwait(0, k)
        accumulate(k, gl, QE, QL)

    def rotate(vectors, rows):
        meansq = jnp.mean(vectors * vectors, axis=-1, keepdims=True)
        normed = vectors * lax.rsqrt(meansq + EPSILON)
        turned = normed * table[0, rows, :] + pltpu.roll(normed, 64, 1) * table[1, rows, :]
        return turned.astype(jnp.bfloat16)

    def halves(step):
        @pl.loop(0, 4)
        def _(m):
            step(pl.ds(pl.multiple_of(m * 128, 128), 128))

    def finish_early(rows):
        ks[rows, :] = rotate(acc[rows, 0:128], rows)
        vs[rows, :] = acc[rows, 128:256].astype(jnp.bfloat16)
        qs[0, rows, :] = rotate(acc[rows, 256:384], rows)
        qs[1, rows, :] = rotate(acc[rows, 384:512], rows)

    def finish_late(heads):
        def step(rows):
            for h in heads:
                qs[h, rows, :] = rotate(acc[rows, QE + 128 * (h - 2) : QE + 128 * (h - 1)], rows)

        halves(step)

    mul = LOG2E / math.sqrt(HEAD_DIM)
    sub = LOG2E * math.sqrt(HEAD_DIM)

    def expo(queries, keys, masked):
        scores = lax.dot_general(queries, keys, NT, preferred_element_type=jnp.float32)
        value = jnp.exp2(scores * mul - sub)
        if masked:
            row = lax.broadcasted_iota(jnp.int32, value.shape, 0)
            col = lax.broadcasted_iota(jnp.int32, value.shape, 1)
            value = jnp.where(row >= col, value, 0.0)
        return value

    def attend(h):
        cols = slice(h * 128, h * 128 + 128)
        e = expo(qs[h, 0:256, :], ks[0:256, :], True)
        mixed = jnp.dot(e.astype(jnp.bfloat16), vs[0:256, :], preferred_element_type=jnp.float32)
        mx[0:256, cols] = (mixed * (1.0 / jnp.sum(e, axis=-1, keepdims=True))).astype(jnp.bfloat16)
        queries = qs[h, 256:512, :]
        e0 = expo(queries, ks[0:256, :], False)
        e1 = expo(queries, ks[256:512, :], True)
        mixed = jnp.dot(e0.astype(jnp.bfloat16), vs[0:256, :], preferred_element_type=jnp.float32)
        mixed = mixed + jnp.dot(e1.astype(jnp.bfloat16), vs[256:512, :], preferred_element_type=jnp.float32)
        r = 1.0 / (jnp.sum(e0, axis=-1, keepdims=True) + jnp.sum(e1, axis=-1, keepdims=True))
        mx[256:512, cols] = (mixed * r).astype(jnp.bfloat16)

    def to_owner(k, slot, quarter, owner):
        j = lax.rem(owner + YN - t, YN) - 1
        remote(pb.at[slot], rb.at[j, quarter], ps.at[0], pr.at[j, quarter], (s, f, owner)).start()

    def partial(k, x):
        pair = pair_of(k)
        quarter = lax.rem(pair, 4)
        b = pl.ds(x * ZN + 2 * pair, 2)
        value = lax.dot_general(mx[:, 0:OE], oe[b].reshape(128, OE), NT, preferred_element_type=jnp.float32)
        value = value + lax.dot_general(mx[:, OE:], ol[b].reshape(128, OL), NT, preferred_element_type=jnp.float32)
        value = value.astype(jnp.bfloat16)
        owner = 2 * x + pair // 4
        slot = 2 * (k - 1) + x

        @pl.when(owner == t)
        def _():
            po[pl.ds(quarter, 1)] = value[None]

        @pl.when(owner != t)
        def _():
            pb[pl.ds(slot, 1)] = value[None]
            if k == 8:
                to_owner(k, slot, quarter, owner)

        if k < 8:
            @pl.when(owner == ydev(2))
            def _():
                for side in (0, 1):
                    half = pb.at[slot, pl.ds(256 * side, 256)]
                    remote(half, rl.at[k - 1, side], ps.at[0], rr.at[k - 1, side], (s, f, ydev(1 + 2 * side))).start()

    def near(k):
        partial(k, xh)

    def far(k):
        if k == 1:
            xwait(1, 0)
        xwait(1, k)
        partial(k, xo)

    def relay(k, x):
        pair = pair_of(k)
        owner = 2 * x + pair // 4
        slot = 2 * (k - 1) + x
        for side in (0, 1):
            @pl.when(owner == ydev(1 + 2 * side))
            def _():
                dst = rl.at[k - 1, side]
                remote(dst, dst, ps.at[0], rr.at[k - 1, side], (s, f, owner)).wait_recv()
                rows = slice(256 * side, 256 * side + 256)
                total = pb[slot, rows, :].astype(jnp.float32) + rl[k - 1, side].astype(jnp.float32)
                pb[pl.ds(slot, 1), rows, :] = total.astype(jnp.bfloat16)[None]
                to_owner(k, slot, lax.rem(pair, 4), owner)

    for k in range(1, 8):
        for i in (0, 2):
            forward(i, k)
        if k > 4:
            accumulate(EARLY[k][0], ge, 0, QE)
        forward(1, k)
        if k == 6:
            early_o.wait_recv()
            for i in (3, 4, 6, 5):
                zsend(i, 1, 1)
                zsend(i, -1, 1)
        if k == 4:
            loads[0].wait()
            for copy in yin:
                copy.wait_recv()
            normalise()
            accumulate(1, ge, 0, QE)
            accumulate_late(1)
        if k > 4:
            accumulate_late(EARLY[k][0])
            for i in EARLY[k][1:]:
                accumulate(i, ge, 0, QE)
                accumulate_late(i)

    forward(3, 1)
    forward(4, 1, crossing=False)
    forward(6, 1, crossing=False)
    forward(0, 8)
    forward(5, 1)
    forward(2, 8)
    accumulate(7, ge, 0, QE)
    forward(1, 8)
    for i in (4, 6):
        xsend(i, 0, 0)
        cross(i, 1)
    accumulate(8, ge, 0, QE)
    loads[1].wait()
    halves(finish_early)
    accumulate_late(7)
    attend(0)
    forward(3, 2)
    attend(1)
    forward(4, 2)
    forward(6, 2)
    forward(5, 2)
    accumulate_late(8)
    finish_late((2, 3, 4))
    forward(3, 3)
    attend(2)
    forward(4, 3)
    finish_late((5, 6, 7))
    forward(6, 3)
    attend(3)
    forward(5, 3)
    attend(4)
    attend(5)
    forward(3, 4)
    attend(6)
    attend(7)
    near(1)
    forward(4, 4)
    far(1)
    forward(6, 4)
    near(2)
    forward(5, 4)
    far(2)
    forward(3, 5)
    forward(4, 5)
    forward(6, 5)
    near(3)
    forward(5, 5)
    relay(1, xh)
    forward(3, 6)
    far(3)
    relay(1, xo)
    forward(4, 6)
    relay(2, xh)
    forward(6, 6)
    near(4)
    forward(5, 6)
    relay(2, xo)
    forward(4, 7)
    far(4)
    relay(3, xh)
    forward(6, 7)
    near(5)
    forward(3, 7)
    relay(3, xo)
    forward(5, 7)
    forward(4, 8)
    far(5)
    relay(4, xh)
    forward(6, 8)
    near(6)
    forward(3, 8)
    relay(4, xo)
    forward(5, 8)
    near(7)
    near(8)
    far(6)
    relay(5, xh)
    relay(5, xo)
    relay(6, xh)
    far(7)
    relay(7, xh)
    relay(6, xo)
    far(8)
    relay(7, xo)

    for k in range(1, 9):
        pair = pair_of(k)
        quarter = lax.rem(pair, 4)

        @pl.when(pair // 4 == lax.rem(t, 2))
        def _():
            sources = (0, 2) if k < 8 else (0, 2, 1)
            for j in sources:
                dst = rb.at[j, quarter]
                remote(dst, dst, ps.at[0], pr.at[j, quarter], (s, f, ydev(1))).wait_recv()
            cols = pl.ds(pl.multiple_of(quarter * 128, 128), 128)
            total = po[quarter].astype(jnp.float32)
            for j in sources:
                total = total + rb[j, quarter].astype(jnp.float32)
            out_ref[:, cols] = (ent[t, :, cols].astype(jnp.float32) + total).astype(jnp.bfloat16)

    def left(ref, sem):
        remote(ref, ref, sem, raw_r.at[0], (s, fpar, t)).wait_send()

    left(ge.at[pl.ds(0, 11)], raw_s.at[0])
    left(ent.at[pl.ds(0, 3)], ya_s.at[0])
    early_o.wait_send()
    for i, (buf, _, _, row, rows) in enumerate(streams):
        left(buf.at[pl.ds(0, 15), pl.ds(row, rows)], zs.at[i])
    for late, buf in enumerate((gl, ol)):
        left(buf.at[pl.ds(0, 16)], xs.at[late])
    left(pb.at[pl.ds(0, 12)], ps.at[0])


def body(entering, w_query, w_keyval, w_out):
    bf16, f32, vmem, dma = jnp.bfloat16, jnp.float32, pltpu.VMEM, pltpu.SemaphoreType.DMA
    operands = (
        entering[0], w_query[0], w_keyval.reshape(ROWS, 256), jnp.swapaxes(w_out[0], 0, 1), jnp.asarray(rope_tables())
    )
    out = pl.pallas_call(
        kernel,
        out_shape=jax.ShapeDtypeStruct((SEQ, FEAT), bf16),
        in_specs=[pl.BlockSpec(memory_space=pl.ANY)] * len(operands),
        out_specs=pl.BlockSpec(memory_space=vmem),
        scratch_shapes=[
            vmem((YN, SEQ, FEAT), bf16), vmem((16, SEQ, 128), bf16), vmem((2, SEQ, HEAD_DIM), f32),
            vmem((4, ROWS, QE), bf16), vmem((2, ROWS, QL), bf16), vmem((2, ROWS, OE + OL), bf16),
            vmem((2 * ZN, ROWS, QE), bf16), vmem((2 * ZN, ROWS, QL), bf16),
            vmem((2 * ZN, ROWS, OE), bf16), vmem((2 * ZN, ROWS, OL), bf16),
            vmem((SEQ, QE + QL), f32),
            vmem((8, SEQ, HEAD_DIM), bf16), vmem((SEQ, HEAD_DIM), bf16), vmem((SEQ, HEAD_DIM), bf16),
            vmem((SEQ, OE + OL), bf16), vmem((16, SEQ, 128), bf16), vmem((4, SEQ, 128), bf16),
            vmem((3, 4, SEQ, 128), bf16), vmem((7, 2, 256, 128), bf16),
            dma((2,)), dma((1,)), dma((8,)), dma((1,)), dma((3,)), dma((7,)), dma((4, 15)),
            dma((2,)), dma((2, 9)), dma((1,)), dma((1,)), dma((1,)), dma((3, 4)), dma((7, 2)),
        ],
        compiler_params=pltpu.CompilerParams(
            collective_id=0, has_side_effects=True, vmem_limit_bytes=40 * 1024 * 1024
        ),
        name="section",
    )(*(pltpu.with_memory_space_constraint(value, pltpu.HBM) for value in operands))
    return out[None]


def solution(mesh):
    in_specs = (
        P("section", "fsdp", "tensor"),
        P("section", "fsdp", "tensor"),
        P("section", "fsdp", "tensor", None),
        P("section", "tensor", "fsdp"),
    )
    out_specs = P("section", "fsdp", "tensor")
    return jax.shard_map(body, mesh=mesh, in_specs=in_specs, out_specs=out_specs, check_vma=False)
```
